32 devices in a mesh: slab: 4 (over y, x), grp: 8 (over z, core).
Axes of the slice: x: 2, y: 2, z: 4, core: 2. Of those that a mesh axis runs over, the one named last changes fastest.
Arguments:
- cell_density: float32 [4, 16, 2, 8], P('slab', 'grp'), may hold values from 1 to 10
- cell_slot: int32 [4, 16, 2, 8], P('slab', 'grp'), may hold values from 0 to 7, each once within a row
- neighbours: int32 [4, 16, 2, 6], P('slab', 'grp'), may hold values from -1 to 127, as said below
- face_code: int32 [4, 16, 2, 6], P('slab', 'grp'), may hold values from 0 to 15, as said below
- stiffness: float32 [64, 64], replicated, as said below
- prolong: float32 [8, 64, 64], replicated, as said below
- penalty: float32 [16, 64, 64], replicated, as said below
- fine_rhs: bfloat16 [4, 16, 2, 8, 4096], P('slab', 'grp'), may hold values from -24 to 24
Outputs:
- coarse_correction: float32 [4, 16, 2, 4096], P(None, 'grp')
The draws below stay inside these ranges and needn't reach their ends.
Inputs may be any that keep to these rules, and one draw needn't show every extreme that they name: `neighbours`: aggregates form a lattice of 4 x 16 x 2; faces in the order -first, +first, -second, +second, -third, +third dimension. Each entry is the number of the lattice neighbour across that face, or -1 where the face lies on the lattice boundary or is a wall; a wall seen from one side is a wall from the other. `face_code`: equal on both sides of every face that is not -1 in neighbours. `cell_slot`: the 8 cells of each aggregate hold each slot once. `stiffness`: Symmetric, each diagonal entry larger than the sum of the magnitudes of the other entries of its row. `prolong`: each diagonal entry larger than the sum of the magnitudes of the other entries of its row. `penalty`: Symmetric, each diagonal entry larger than the sum of the magnitudes of the other entries of its row.
All inputs are finite; a program needn't handle non-finite values.
Results may differ from the reference program's by a relative error of at most 0.0003.
Values sent between devices are 32-bit elements; how exact they have to be, the bound alone decides.
No kernel may reach another device: no remote copies, remote signals or barrier semaphores. Data moves between devices by JAX's collectives and lax.ppermute only.
A program may use at most 128 MiB of HBM per device.

```python
import math
import jax
import jax.numpy as jnp
from jax import lax

DOF = 64
NRHS = 64
KIDS = 8
NCODE = 16
SWEEPS = 8
LC = 2
AX = 4
BX = 16


def lattice_faces(key):
    walls = jax.random.randint(jax.random.fold_in(key, 11), (3, AX, BX, LC), 0, 4) == 0
    pattern = jax.random.randint(jax.random.fold_in(key, 12), (AX, BX, LC), 0, NCODE)
    first_idx = lax_iota(0)
    second_idx = lax_iota(1)
    third_idx = lax_iota(2)
    flat = (first_idx * BX + second_idx) * LC + third_idx
    sizes_all = (AX, BX, LC)
    strides = (BX * LC, LC, 1)
    places = (first_idx, second_idx, third_idx)
    links = []
    codes = []
    for axis in range(3):
        down_open = (places[axis] > 0) & jnp.logical_not(jnp.roll(walls[axis], 1, axis=axis))
        up_open = (places[axis] + 1 < sizes_all[axis]) & jnp.logical_not(walls[axis])
        links.append(jnp.where(down_open, flat - strides[axis], -1))
        links.append(jnp.where(up_open, flat + strides[axis], -1))
        codes.append((pattern + jnp.roll(pattern, 1, axis=axis)) % NCODE)
        codes.append((pattern + jnp.roll(pattern, -1, axis=axis)) % NCODE)
    return (jnp.stack(links, axis=-1).astype(jnp.int32), jnp.stack(codes, axis=-1).astype(jnp.int32))


def lax_iota(axis):
    shape = (AX, BX, LC)
    return jax.lax.broadcasted_iota(jnp.int32, shape, axis)


def draw_neighbours(key, part):
    return lattice_faces(key)[0]


def draw_face_code(key, part):
    return lattice_faces(key)[1]


def dominant(key, lead, size, bound, base, spread, symmetric):
    raw = jax.random.uniform(jax.random.fold_in(key, 21), lead + (size, size), jnp.float32, -bound, bound)
    if symmetric:
        raw = 0.5 * (raw + jnp.swapaxes(raw, -1, -2))
    eye = jnp.eye(size, dtype=jnp.float32)
    centre = base + jax.random.uniform(jax.random.fold_in(key, 22), lead + (size, 1), jnp.float32, 0.0, spread)
    return raw * (1.0 - eye) + eye * centre


def draw_stiffness(key, part):
    return dominant(key, (), DOF, 1.8 / DOF, 3.0, 1.0, True)


def draw_prolong(key, part):
    return dominant(key, (KIDS,), DOF, 0.9 / DOF, 1.0, 0.5, False)


def draw_penalty(key, part):
    return dominant(key, (NCODE,), DOF, 1.8 / DOF, 3.0, 2.0, True)


def block_scale(stream_key, shape, shards, low, high):
    level, own = 1.0, jax.random.fold_in(stream_key, 6)
    for axis_at, shards_of in shards:
        heights = jnp.exp(jax.random.uniform(jax.random.fold_in(own, axis_at), (shards_of,), jnp.float32, low / len(shards), high / len(shards)))
        level = level * jnp.repeat(heights, shape[axis_at] // shards_of).reshape([-1 if axis == axis_at else 1 for axis in range(len(shape))])
    return level


def centred(rng, dims, scale, reach, cuts=(), held_as=jnp.bfloat16):
    array = jax.random.normal(rng, dims, jnp.float32) * scale
    if len(cuts) > 0:
        array = block_scale(rng, dims, cuts, -0.22, 0.18) * array
    return jnp.clip(array, min=-reach, max=reach).astype(held_as)


def setup_inputs(seed: int = 0) -> dict:
    streams_of = jax.random.split(jax.random.key(seed), 9)
    cell_density = jnp.clip(jnp.exp(math.log(10.0) - 2.3025851 * jax.random.uniform(streams_of[0], (AX, BX, LC, KIDS), jnp.float32) ** block_scale(streams_of[0], (AX, BX, LC, KIDS), ((0, 4), (1, 8)), -0.2, 0.2)), 1.0, 10.0)
    cell_slot = jax.vmap(lambda own: jax.random.permutation(own, KIDS))(jax.random.split(streams_of[1], AX * BX * LC)).reshape((AX, BX, LC, KIDS)).astype(jnp.int32)
    neighbours = draw_neighbours(jax.random.fold_in(streams_of[8], 71), 0)
    face_code = draw_face_code(jax.random.fold_in(streams_of[8], 71), 0)
    stiffness = draw_stiffness(jax.random.fold_in(streams_of[8], 71), 0)
    prolong = draw_prolong(jax.random.fold_in(streams_of[8], 71), 0)
    penalty = draw_penalty(jax.random.fold_in(streams_of[8], 71), 0)
    fine_rhs = centred(streams_of[7], (AX, BX, LC, KIDS, DOF * NRHS), 4.0, 24.0, ((0, 4), (1, 8)))
    return {"cell_density": cell_density, "cell_slot": cell_slot, "neighbours": neighbours, "face_code": face_code, "stiffness": stiffness, "prolong": prolong, "penalty": penalty, "fine_rhs": fine_rhs}


def reference(cell_density, cell_slot, neighbours, face_code, stiffness, prolong, penalty, fine_rhs):
    highest = lax.Precision.HIGHEST
    count = AX * BX * LC
    templates = jnp.einsum('sji,jk,skl->sil', prolong, stiffness, prolong, precision=highest)
    density = cell_density.reshape(count, KIDS)
    slots = cell_slot.reshape(count, KIDS)
    links = neighbours.reshape(count, 6)
    codes = face_code.reshape(count, 6)
    mean_rho = jnp.mean(density, axis=1)
    onehot = (slots[:, :, None] == jnp.arange(KIDS, dtype=jnp.int32)[None, None, :]).astype(jnp.float32)
    weights = jnp.einsum('aq,aqs->as', 1.0 / density, onehot, precision=highest)
    present = links >= 0
    safe_links = jnp.where(present, links, 0).astype(jnp.int32)
    others = mean_rho[safe_links]
    face_weight = jnp.where(present, 2.0 / (mean_rho[:, None] + others), jnp.float32(0.0))
    code_hot = (codes[:, :, None] == jnp.arange(NCODE, dtype=jnp.int32)[None, None, :]).astype(jnp.float32) * face_weight[:, :, None]
    flat_templ = templates.reshape(KIDS, DOF * DOF)
    flat_pen = penalty.reshape(NCODE, DOF * DOF)
    cell_part = jnp.dot(weights, flat_templ, precision=highest)
    face_part = jnp.dot(jnp.sum(code_hot, axis=1), flat_pen, precision=highest)
    diag_blocks = (cell_part + face_part).reshape(count, DOF, DOF)
    off_blocks = (-jnp.dot(code_hot.reshape(count * 6, NCODE), flat_pen, precision=highest)).reshape(count, 6, DOF, DOF)
    cell_prolong = prolong[slots]
    cell_rhs = fine_rhs.reshape(count, KIDS, DOF, NRHS).astype(jnp.float32)
    coarse_rhs = jnp.einsum('aqji,aqjr->air', cell_prolong, cell_rhs, precision=highest)
    jacobi = jnp.diagonal(diag_blocks, axis1=1, axis2=2)
    totals = jnp.sum(jnp.abs(diag_blocks), axis=2) + jnp.sum(jnp.abs(off_blocks), axis=(1, 3))
    upper = jnp.max(totals / jacobi)
    jacobi = jacobi[:, :, None]
    gather_index = jnp.where(present, links, count).astype(jnp.int32)

    def apply_op(vector):
        result = jnp.einsum('aij,ajr->air', diag_blocks, vector, precision=highest)
        padded = jnp.concatenate([vector, jnp.zeros((1, DOF, NRHS), jnp.float32)], axis=0)
        for face in range(6):
            result = result + jnp.einsum('aij,ajr->air', off_blocks[:, face], padded[gather_index[:, face]], precision=highest)
        return result

    lower = upper / 10.0
    centre_val = 0.5 * (upper + lower)
    half_width = 0.5 * (upper - lower)
    sigma_val = centre_val / half_width
    damping = 1.0 / sigma_val
    resid = coarse_rhs
    update = resid / jacobi / centre_val
    solution = update
    for sweep in range(SWEEPS):
        resid = resid - apply_op(update)
        damping_next = 1.0 / (2.0 * sigma_val - damping)
        update = damping_next * damping * update + (2.0 * damping_next / half_width) * (resid / jacobi)
        solution = solution + update
        damping = damping_next
    return solution.reshape(AX, BX, LC, DOF * NRHS)
```

```python
import jax
import jax.numpy as jnp
from jax import lax
from jax.experimental import pallas as pl
from jax.experimental.pallas import tpu as pltpu
from jax.sharding import PartitionSpec as P

SWEEPS = 8
LANES = 128
FACES = 6
PADM = 32
GROUPS = 4

f32 = jnp.float32
bf16 = jnp.bfloat16


def halves(x):
    hi = x.astype(bf16)
    lo = (x - hi.astype(f32)).astype(bf16)
    return hi, lo


def contract0(a, b):
    return lax.dot_general(a, b, (((0,), (0,)), ((), ())), preferred_element_type=f32)


def coarse_kernel(slot_s, dens, slot_v, links, code, prolong, rhs, out, pairs, info):
    kids, dof, _ = prolong.shape
    half = dof // 2
    _, rows_b, rows_c, _ = dens.shape
    count = rows_b * rows_c
    groups = rhs.shape[2] // 4
    for s in range(kids):
        even = prolong[s, pl.ds(0, half, stride=2), :]
        odd = prolong[s, pl.ds(1, half, stride=2), :]
        hi, lo = halves(jnp.concatenate([even, odd], axis=1))
        pairs[s] = jnp.concatenate([hi, lo], axis=1)
    info[...] = jnp.zeros(info.shape, f32)
    for a in range(count):
        b, c = a // rows_c, a % rows_c
        info[a : a + 1, 0:kids] = dens[0, b, c : c + 1, :]
        info[a : a + 1, kids : 2 * kids] = slot_v[0, b, c : c + 1, :].astype(f32)
        info[a : a + 1, 2 * kids : 2 * kids + FACES] = jnp.where(
            links[0, b, c : c + 1, :] >= 0, f32(1.0), f32(0.0)
        )
        info[a : a + 1, 3 * kids : 3 * kids + FACES] = code[0, b, c : c + 1, :].astype(f32)
    members = out.shape[0]
    for a in range(count):
        b, c = a // rows_c, a % rows_c
        weights = jnp.concatenate([pairs[slot_s[0, b, c, q]] for q in range(kids)], axis=0)
        prod = contract0(rhs[a], weights)
        prod = prod[:, :LANES] + prod[:, LANES:]
        own = prod[:dof, :dof] + prod[dof:, dof:]
        row = jnp.concatenate([own[:groups], own[groups:]], axis=1)
        for first in range(0, members, groups):
            out[first : first + groups, a, :] = row
    out[:, count : 2 * count, :] = jnp.broadcast_to(info[0:count, :][None], (members, count, LANES))


def matrices_kernel(stiffness, prolong, penalty, stacked, columns, mall, extra):
    kids, dof, _ = prolong.shape
    codes = penalty.shape[0]
    s_hi, s_lo = halves(stiffness[...])
    s_left = jnp.concatenate([s_hi, s_hi, s_lo], axis=1)
    for s in range(kids):
        p_hi, p_lo = halves(prolong[s])
        sp = jnp.dot(s_left, jnp.concatenate([p_hi, p_lo, p_hi], axis=0), preferred_element_type=f32)
        q_hi, q_lo = halves(sp)
        mall[s] = contract0(
            jnp.concatenate([p_hi, p_hi, p_lo], axis=0), jnp.concatenate([q_hi, q_lo, q_hi], axis=0)
        )
    mall[kids : kids + codes] = penalty[...]
    mall[kids + codes :] = jnp.zeros((PADM - kids - codes, dof, dof), f32)
    rows = dof // GROUPS
    eye = (
        lax.broadcasted_iota(jnp.int32, (dof, dof), 0) == lax.broadcasted_iota(jnp.int32, (dof, dof), 1)
    ).astype(f32)
    extra[...] = jnp.zeros(extra.shape, f32)
    for m in range(kids + codes):
        mat = mall[m]
        hi, lo = halves(mat)
        wide = jnp.concatenate([hi, hi, lo], axis=1)
        for g in range(GROUPS):
            stacked[g, m * rows : (m + 1) * rows, :] = wide[g * rows : (g + 1) * rows]
        extra[m : m + 1, 0:dof] = jnp.sum(mat * eye, axis=0, keepdims=True)
        if m >= kids:
            extra[m : m + 1, dof : 2 * dof] = jnp.sum(jnp.abs(mat), axis=0, keepdims=True)
    for pair in range(dof // 2 + 1):
        if pair < dof // 2:
            both = jnp.concatenate([mall[:, 2 * pair, :], mall[:, 2 * pair + 1, :]], axis=1)
        else:
            both = extra[...]
        hi, lo = halves(both.T)
        columns[pair] = jnp.concatenate([hi, hi, lo], axis=1)


def solve_kernel(strides, got, stacked, columns, out, flat, resid, update, answer, coefs, tiles):
    count = got.shape[1] // 2
    members = got.shape[0]
    total = members * count
    dof = resid.shape[0]
    kids = 8
    rows = dof // GROUPS
    for a in range(count):
        flat[0, pl.ds(a, members, stride=count), :] = got[:, a, :]
        flat[1, pl.ds(a, members, stride=count), :] = got[:, count + a, :]
    coarse = flat[0].T
    facts = flat[1].T
    dens = facts[0:kids]
    slots = facts[kids : 2 * kids]
    open_face = facts[2 * kids : 2 * kids + FACES] > 0.5
    codes = facts[3 * kids : 3 * kids + FACES].astype(jnp.int32)
    rho = jnp.sum(dens, axis=0, keepdims=True) * f32(1.0 / kids)
    inverse = 1.0 / dens
    place = lax.broadcasted_iota(jnp.int32, (kids, total), 0).astype(f32)
    weight = jnp.zeros((kids, total), f32)
    for q in range(kids):
        weight = weight + jnp.where(slots[q : q + 1] == place, inverse[q : q + 1], 0.0)
    shifts = [sign * stride for stride in strides for sign in (-1, 1)]
    code_place = lax.broadcasted_iota(jnp.int32, (16, total), 0)
    face_sum = jnp.zeros((16, total), f32)
    face_w = []
    for f in range(FACES):
        other = pltpu.roll(rho, (-shifts[f]) % total, 1)
        fw = jnp.where(open_face[f : f + 1], 2.0 / (rho + other), 0.0)
        face_w.append(fw)
        face_sum = face_sum + jnp.where(codes[f : f + 1] == code_place, fw, 0.0)
    coef = jnp.concatenate([weight, face_sum, jnp.zeros((8, total), f32)], axis=0)
    c_hi, c_lo = halves(coef)
    c_all = jnp.concatenate([c_hi, c_lo, c_hi], axis=0)
    last = jnp.dot(columns[dof // 2], c_all, preferred_element_type=f32)
    jacobi = last[:dof]
    sums = last[dof:]
    for pair in range(dof // 2):
        part = jnp.abs(jnp.dot(columns[pair], c_all, preferred_element_type=f32))
        sums = sums + (part[:dof] + part[dof:])
    upper = jnp.max(jnp.max(sums / jacobi, axis=0, keepdims=True), axis=1, keepdims=True)
    lower = upper / 10.0
    centre = 0.5 * (upper + lower)
    half_width = 0.5 * (upper - lower)
    sigma = centre / half_width
    damping = 1.0 / sigma
    inv_jac = 1.0 / jacobi
    inv_jac = jnp.concatenate([inv_jac, inv_jac], axis=1)
    start = jnp.concatenate([coarse[:dof], coarse[dof:]], axis=1)
    resid[...] = start
    start = start * inv_jac / centre
    update[...] = start
    answer[...] = start
    for f in range(FACES):
        coefs[f : f + 1, :] = jnp.concatenate([face_w[f], face_w[f]], axis=1)
        fc = codes[f : f + 1].astype(f32)
        coefs[8 + f : 9 + f, :] = jnp.concatenate([fc, fc], axis=1)
    coefs[16:24, :] = jnp.concatenate([weight, weight], axis=1)
    jac2 = inv_jac

    def sweep(_, damp):
        hi, lo = halves(update[...])
        right = jnp.concatenate([hi, lo, hi], axis=0)
        damp_next = 1.0 / (2.0 * sigma - damp)
        keep = damp_next * damp
        gain = 2.0 * damp_next / half_width
        for g in range(GROUPS):
            prod = jnp.dot(stacked[g], right, preferred_element_type=f32)
            mats = [prod[m * rows : (m + 1) * rows] for m in range(24)]
            applied = coefs[16:17] * mats[0]
            for s in range(1, kids):
                applied = applied + coefs[16 + s : 17 + s] * mats[s]
            terms = []
            for f in range(FACES):
                fc = coefs[8 + f : 9 + f].astype(jnp.int32)
                fc = jnp.broadcast_to(fc, (rows, 2 * total))
                level = mats[kids:]
                for bit in range(4):
                    on = ((fc >> bit) & 1) > 0
                    level = [
                        jnp.where(on, level[2 * n + 1], level[2 * n]) for n in range(len(level) // 2)
                    ]
                terms.append(coefs[f : f + 1] * level[0])
            for f in range(FACES):
                moved = terms[f ^ 1]
                moved = jnp.concatenate(
                    [
                        pltpu.roll(moved[:, :total], (-shifts[f]) % total, 1),
                        pltpu.roll(moved[:, total:], (-shifts[f]) % total, 1),
                    ],
                    axis=1,
                )
                applied = applied + (terms[f] - moved)
            part = pl.ds(g * rows, rows)
            left = resid[part, :] - applied
            resid[part, :] = left
            new = keep * update[part, :] + gain * (left * jac2[g * rows : (g + 1) * rows])
            update[part, :] = new
            answer[part, :] = answer[part, :] + new
        return damp_next

    lax.fori_loop(0, SWEEPS, sweep, damping)
    grp_count = strides[0] // count
    firsts = total // strides[0]
    half = dof // 2
    lane_tiles = total // LANES
    for t in range(2 * lane_tiles):
        tiles[t] = answer[:, t * LANES : (t + 1) * LANES]
    for low in range(2):
        for c in range(2):
            for t in range(lane_tiles):
                block = tiles[c * lane_tiles + t, pl.ds(low, half, stride=2), :]
                flat[0, t * LANES : (t + 1) * LANES, 0:half] = block.T
            row = jnp.concatenate(
                [flat[0, pl.ds(n, members, stride=count), 0:half] for n in range(count)], axis=1
            )
            for i in range(firsts):
                piece = row[i * grp_count : (i + 1) * grp_count]
                for s in range(members // grp_count):
                    out[pl.ds(s * grp_count, grp_count), (low * 2 + c) * firsts + i, :] = piece


def finish_kernel(got, out):
    firsts = got.shape[1] // 4
    sources = 32
    rows_b, rows_c = 2, 2
    half = 32
    for i in range(firsts):
        block = jnp.concatenate([got[0:sources, x * firsts + i, :] for x in range(4)], axis=0).T
        for n in range(rows_b * rows_c):
            b, c = n // rows_c, n % rows_c
            out[i * rows_b + b, pl.ds(c, half, stride=rows_c), :] = block[n * half : (n + 1) * half]


def vmem():
    return pl.BlockSpec(memory_space=pltpu.VMEM)


def local(cell_density, cell_slot, neighbours, face_code, stiffness, prolong, penalty, fine_rhs):
    _, rows_b, rows_c, kids = cell_density.shape
    dof = stiffness.shape[0]
    count = rows_b * rows_c
    slabs, grps = lax.axis_size("slab"), lax.axis_size("grp")
    members = slabs * grps
    total = members * count
    every = ("slab", "grp")
    strides = (grps * count, rows_c, 1)
    rhs = fine_rhs.reshape(count, kids * dof // 2, LANES)
    sent = pl.pallas_call(
        coarse_kernel,
        out_shape=jax.ShapeDtypeStruct((members, 2 * count, LANES), f32),
        in_specs=[pl.BlockSpec(memory_space=pltpu.SMEM)] + [vmem()] * 6,
        out_specs=vmem(),
        scratch_shapes=[pltpu.VMEM((kids, dof // 2, 2 * LANES), bf16), pltpu.VMEM((8, LANES), f32)],
        name="coarse",
    )(cell_slot, cell_density, cell_slot, neighbours, face_code, prolong, rhs)
    got = lax.all_to_all(sent, every, 0, 0, tiled=True)
    stacked, columns = pl.pallas_call(
        matrices_kernel,
        out_shape=(
            jax.ShapeDtypeStruct((GROUPS, 24 * (dof // GROUPS), 3 * dof), bf16),
            jax.ShapeDtypeStruct((dof // 2 + 1, 2 * dof, 3 * PADM), bf16),
        ),
        in_specs=[vmem()] * 3,
        out_specs=(vmem(), vmem()),
        scratch_shapes=[pltpu.VMEM((PADM, dof, dof), f32), pltpu.VMEM((PADM, 2 * dof), f32)],
        name="matrices",
    )(stiffness, prolong, penalty)
    back = pl.pallas_call(
        lambda *refs: solve_kernel(strides, *refs),
        out_shape=jax.ShapeDtypeStruct((members, 4 * slabs, LANES), f32),
        in_specs=[vmem()] * 3,
        out_specs=vmem(),
        scratch_shapes=[
            pltpu.VMEM((2, total, LANES), f32),
            pltpu.VMEM((dof, 2 * total), f32),
            pltpu.VMEM((dof, 2 * total), f32),
            pltpu.VMEM((dof, 2 * total), f32),
            pltpu.VMEM((24, 2 * total), f32),
            pltpu.VMEM((2 * total // LANES, dof, LANES), f32),
        ],
        name="solve",
    )(got, stacked, columns)
    back = lax.all_to_all(back, every, 0, 0, tiled=True)
    full = pl.pallas_call(
        finish_kernel,
        out_shape=jax.ShapeDtypeStruct((slabs * rows_b, dof, LANES), f32),
        in_specs=[vmem()],
        out_specs=vmem(),
        name="finish",
    )(back)
    full = full.reshape(slabs, rows_b, dof // 2, rows_c, LANES).transpose(0, 1, 3, 2, 4)
    return full.reshape(slabs, rows_b, rows_c, dof // 2 * LANES)


def solution(mesh):
    return jax.shard_map(
        local,
        mesh=mesh,
        in_specs=(
            P("slab", "grp", None, None),
            P("slab", "grp", None, None),
            P("slab", "grp", None, None),
            P("slab", "grp", None, None),
            P(),
            P(),
            P(),
            P("slab", "grp", None, None, None),
        ),
        out_specs=P(None, "grp", None, None),
        check_vma=False,
    )
```

```python
import jax
import jax.numpy as jnp
from jax import lax
from jax.experimental import pallas as pl
from jax.experimental.pallas import tpu as pltpu
from jax.sharding import PartitionSpec as P

SWEEPS = 8
LANES = 128
FACES = 6
PADM = 32
GROUPS = 4

f32 = jnp.float32
bf16 = jnp.bfloat16


def halves(x):
    hi = x.astype(bf16)
    lo = (x - hi.astype(f32)).astype(bf16)
    return hi, lo


def contract0(a, b):
    return lax.dot_general(a, b, (((0,), (0,)), ((), ())), preferred_element_type=f32)


def coarse_kernel(slot_s, dens, slot_v, links, code, prolong, rhs, out, wide, pairs, weights, info):
    kids, dof, _ = prolong.shape
    half = dof // 2
    _, rows_b, rows_c, _ = dens.shape
    count = rows_b * rows_c
    members = out.shape[0]
    groups = half
    info[...] = jnp.zeros(info.shape, f32)
    for a in range(count):
        b, c = a // rows_c, a % rows_c
        info[a : a + 1, 0:kids] = dens[0, b, c : c + 1, :]
        info[a : a + 1, kids : 2 * kids] = slot_v[0, b, c : c + 1, :].astype(f32)
        info[a : a + 1, 2 * kids : 2 * kids + FACES] = jnp.where(
            links[0, b, c : c + 1, :] >= 0, f32(1.0), f32(0.0)
        )
        info[a : a + 1, 3 * kids : 3 * kids + FACES] = code[0, b, c : c + 1, :].astype(f32)
    out[:, count : 2 * count, :] = jnp.broadcast_to(info[0:count, :][None], (members, count, LANES))
    first_half = lax.broadcasted_iota(jnp.int32, (half, LANES), 1) < dof
    for s in range(kids):
        wide[s, :, 0:dof] = prolong[s]
        even = wide[s, pl.ds(0, half, stride=2), :]
        odd = wide[s, pl.ds(1, half, stride=2), :]
        pairs[s] = jnp.where(first_half, even, pltpu.roll(odd, dof, 1))
    for a in range(count):
        b, c = a // rows_c, a % rows_c
        for q in range(kids):
            weights[a, pl.ds(q, half, stride=kids), :] = pairs[slot_s[0, b, c, q]]
    for a in range(count):
        b, c = a // rows_c, a % rows_c
        cells = rhs[0, b, c].astype(f32)
        cells = jnp.concatenate([cells[:, t * LANES : (t + 1) * LANES] for t in range(half)], axis=0)
        hi, lo = halves(weights[a])
        prod = contract0(cells.astype(bf16), jnp.concatenate([hi, lo], axis=1))
        prod = prod[:, :LANES] + prod[:, LANES:]
        own = prod[:dof, :dof] + prod[dof:, dof:]
        row = jnp.concatenate([own[:groups], own[groups:]], axis=1)
        for first in range(0, members, groups):
            out[first : first + groups, a, :] = row


def matrices_kernel(stiffness, prolong, penalty, stacked, columns, mall, extra):
    kids, dof, _ = prolong.shape
    codes = penalty.shape[0]
    half = dof // 2
    rows = dof // GROUPS
    s_hi, s_lo = halves(stiffness[...])
    s_left = jnp.concatenate([s_hi, s_hi, s_lo], axis=1)
    eye = (
        lax.broadcasted_iota(jnp.int32, (dof, dof), 0) == lax.broadcasted_iota(jnp.int32, (dof, dof), 1)
    ).astype(f32)
    extra[...] = jnp.zeros(extra.shape, f32)
    mall[kids + codes :] = jnp.zeros((PADM - kids - codes, half, 2 * dof), f32)
    for m in range(kids + codes):
        if m < kids:
            p_hi, p_lo = halves(prolong[m])
            right = jnp.concatenate([p_hi, p_lo, p_hi], axis=0)
            q_hi, q_lo = halves(jnp.dot(s_left, right, preferred_element_type=f32))
            mat = contract0(
                jnp.concatenate([p_hi, p_hi, p_lo], axis=0), jnp.concatenate([q_hi, q_lo, q_hi], axis=0)
            )
        else:
            mat = penalty[m - kids]
            extra[m : m + 1, dof : 2 * dof] = jnp.sum(jnp.abs(mat), axis=0, keepdims=True)
        extra[m : m + 1, 0:dof] = jnp.sum(mat * eye, axis=0, keepdims=True)
        mall[m, :, 0:dof] = mat[:half]
        mall[m, :, dof : 2 * dof] = mat[half:]
        hi, lo = halves(mat)
        wide = jnp.concatenate([hi, hi, lo], axis=1)
        for g in range(GROUPS):
            stacked[g, m * rows : (m + 1) * rows, :] = wide[g * rows : (g + 1) * rows]
    for pair in range(half + 1):
        hi, lo = halves(mall[:, pair, :] if pair < half else extra[...])
        columns[pair] = jnp.concatenate([hi, hi, lo], axis=0).T


def solve_kernel(strides, got, stacked, columns, out, flat, resid, update, answer, coefs, tiles):
    count = got.shape[1] // 2
    members = got.shape[0]
    total = members * count
    dof = resid.shape[0]
    kids = 8
    rows = dof // GROUPS
    for a in range(count):
        flat[0, pl.ds(a, members, stride=count), :] = got[:, a, :]
        flat[1, pl.ds(a, members, stride=count), :] = got[:, count + a, :]
    coarse = flat[0].T
    facts = flat[1].T
    dens = facts[0:kids]
    slots = facts[kids : 2 * kids]
    open_face = facts[2 * kids : 2 * kids + FACES] > 0.5
    codes = facts[3 * kids : 3 * kids + FACES].astype(jnp.int32)
    rho = jnp.sum(dens, axis=0, keepdims=True) * f32(1.0 / kids)
    inverse = 1.0 / dens
    place = lax.broadcasted_iota(jnp.int32, (kids, total), 0).astype(f32)
    weight = jnp.zeros((kids, total), f32)
    for q in range(kids):
        weight = weight + jnp.where(slots[q : q + 1] == place, inverse[q : q + 1], 0.0)
    shifts = [sign * stride for stride in strides for sign in (-1, 1)]
    code_place = lax.broadcasted_iota(jnp.int32, (16, total), 0)
    face_sum = jnp.zeros((16, total), f32)
    face_w = []
    for f in range(FACES):
        other = pltpu.roll(rho, (-shifts[f]) % total, 1)
        fw = jnp.where(open_face[f : f + 1], 2.0 / (rho + other), 0.0)
        face_w.append(fw)
        face_sum = face_sum + jnp.where(codes[f : f + 1] == code_place, fw, 0.0)
    coef = jnp.concatenate([weight, face_sum, jnp.zeros((8, total), f32)], axis=0)
    c_hi, c_lo = halves(coef)
    c_all = jnp.concatenate([c_hi, c_lo, c_hi], axis=0)
    last = jnp.dot(columns[dof // 2], c_all, preferred_element_type=f32)
    jacobi = last[:dof]
    sums = last[dof:]
    for pair in range(dof // 2):
        part = jnp.abs(jnp.dot(columns[pair], c_all, preferred_element_type=f32))
        sums = sums + (part[:dof] + part[dof:])
    upper = jnp.max(jnp.max(sums / jacobi, axis=0, keepdims=True), axis=1, keepdims=True)
    lower = upper / 10.0
    centre = 0.5 * (upper + lower)
    half_width = 0.5 * (upper - lower)
    sigma = centre / half_width
    damping = 1.0 / sigma
    inv_jac = 1.0 / jacobi
    inv_jac = jnp.concatenate([inv_jac, inv_jac], axis=1)
    start = jnp.concatenate([coarse[:dof], coarse[dof:]], axis=1)
    resid[...] = start
    start = start * inv_jac / centre
    update[...] = start
    answer[...] = start
    for f in range(FACES):
        coefs[f : f + 1, :] = jnp.concatenate([face_w[f], face_w[f]], axis=1)
        fc = codes[f : f + 1].astype(f32)
        coefs[8 + f : 9 + f, :] = jnp.concatenate([fc, fc], axis=1)
    coefs[16:24, :] = jnp.concatenate([weight, weight], axis=1)
    jac2 = inv_jac

    def sweep(_, damp):
        hi, lo = halves(update[...])
        right = jnp.concatenate([hi, lo, hi], axis=0)
        damp_next = 1.0 / (2.0 * sigma - damp)
        keep = damp_next * damp
        gain = 2.0 * damp_next / half_width
        for g in range(GROUPS):
            prod = jnp.dot(stacked[g], right, preferred_element_type=f32)
            mats = [prod[m * rows : (m + 1) * rows] for m in range(24)]
            applied = coefs[16:17] * mats[0]
            for s in range(1, kids):
                applied = applied + coefs[16 + s : 17 + s] * mats[s]
            terms = []
            for f in range(FACES):
                fc = coefs[8 + f : 9 + f].astype(jnp.int32)
                fc = jnp.broadcast_to(fc, (rows, 2 * total))
                level = mats[kids:]
                for bit in range(4):
                    on = ((fc >> bit) & 1) > 0
                    level = [
                        jnp.where(on, level[2 * n + 1], level[2 * n]) for n in range(len(level) // 2)
                    ]
                terms.append(coefs[f : f + 1] * level[0])
            for f in range(FACES):
                moved = terms[f ^ 1]
                moved = jnp.concatenate(
                    [
                        pltpu.roll(moved[:, :total], (-shifts[f]) % total, 1),
                        pltpu.roll(moved[:, total:], (-shifts[f]) % total, 1),
                    ],
                    axis=1,
                )
                applied = applied + (terms[f] - moved)
            part = pl.ds(g * rows, rows)
            left = resid[part, :] - applied
            resid[part, :] = left
            new = keep * update[part, :] + gain * (left * jac2[g * rows : (g + 1) * rows])
            update[part, :] = new
            answer[part, :] = answer[part, :] + new
        return damp_next

    lax.fori_loop(0, SWEEPS, sweep, damping)
    grp_count = strides[0] // count
    firsts = total // strides[0]
    half = dof // 2
    lane_tiles = total // LANES
    for t in range(2 * lane_tiles):
        tiles[t] = answer[:, t * LANES : (t + 1) * LANES]
    for low in range(2):
        for c in range(2):
            for t in range(lane_tiles):
                block = tiles[c * lane_tiles + t, pl.ds(low, half, stride=2), :]
                flat[0, t * LANES : (t + 1) * LANES, 0:half] = block.T
            row = jnp.concatenate(
                [flat[0, pl.ds(n, members, stride=count), 0:half] for n in range(count)], axis=1
            )
            for i in range(firsts):
                piece = row[i * grp_count : (i + 1) * grp_count]
                for s in range(members // grp_count):
                    out[pl.ds(s * grp_count, grp_count), (low * 2 + c) * firsts + i, :] = piece


def finish_kernel(got, out):
    firsts = got.shape[1] // 4
    sources = 32
    rows_b, rows_c = 2, 2
    half = 32
    for i in range(firsts):
        block = jnp.concatenate([got[0:sources, x * firsts + i, :] for x in range(4)], axis=0).T
        for n in range(rows_b * rows_c):
            b, c = n // rows_c, n % rows_c
            out[i * rows_b + b, pl.ds(c, half, stride=rows_c), :] = block[n * half : (n + 1) * half]


def vmem():
    return pl.BlockSpec(memory_space=pltpu.VMEM)


def near(x):
    return pltpu.with_memory_space_constraint(x, pltpu.VMEM)


def local(cell_density, cell_slot, neighbours, face_code, stiffness, prolong, penalty, fine_rhs):
    _, rows_b, rows_c, kids = cell_density.shape
    dof = stiffness.shape[0]
    count = rows_b * rows_c
    slabs, grps = lax.axis_size("slab"), lax.axis_size("grp")
    members = slabs * grps
    total = members * count
    every = ("slab", "grp")
    strides = (grps * count, rows_c, 1)
    sent = pl.pallas_call(
        coarse_kernel,
        out_shape=pltpu.VMEM((members, 2 * count, LANES), f32),
        in_specs=[pl.BlockSpec(memory_space=pltpu.SMEM)] + [vmem()] * 6,
        out_specs=vmem(),
        scratch_shapes=[
            pltpu.VMEM((kids, dof, LANES), f32),
            pltpu.VMEM((kids, dof // 2, LANES), f32),
            pltpu.VMEM((count, kids * dof // 2, LANES), f32),
            pltpu.VMEM((8, LANES), f32),
        ],
        name="coarse",
    )(cell_slot, cell_density, cell_slot, neighbours, face_code, prolong, fine_rhs)
    got = lax.all_to_all(sent, every, 0, 0, tiled=True)
    stacked, columns = pl.pallas_call(
        matrices_kernel,
        out_shape=(
            pltpu.VMEM((GROUPS, 24 * (dof // GROUPS), 3 * dof), bf16),
            pltpu.VMEM((dof // 2 + 1, 2 * dof, 3 * PADM), bf16),
        ),
        in_specs=[vmem()] * 3,
        out_specs=(vmem(), vmem()),
        scratch_shapes=[pltpu.VMEM((PADM, dof // 2, 2 * dof), f32), pltpu.VMEM((PADM, 2 * dof), f32)],
        compiler_params=pltpu.CompilerParams(vmem_limit_bytes=24 << 20),
        name="matrices",
    )(near(stiffness), near(prolong), near(penalty))
    back = pl.pallas_call(
        lambda *refs: solve_kernel(strides, *refs),
        out_shape=pltpu.VMEM((members, 4 * slabs, LANES), f32),
        in_specs=[vmem()] * 3,
        out_specs=vmem(),
        scratch_shapes=[
            pltpu.VMEM((2, total, LANES), f32),
            pltpu.VMEM((dof, 2 * total), f32),
            pltpu.VMEM((dof, 2 * total), f32),
            pltpu.VMEM((dof, 2 * total), f32),
            pltpu.VMEM((24, 2 * total), f32),
            pltpu.VMEM((2 * total // LANES, dof, LANES), f32),
        ],
        compiler_params=pltpu.CompilerParams(vmem_limit_bytes=40 << 20),
        name="solve",
    )(near(got), near(stacked), near(columns))
    back = lax.all_to_all(back, every, 0, 0, tiled=True)
    full = pl.pallas_call(
        finish_kernel,
        out_shape=jax.ShapeDtypeStruct((slabs * rows_b, dof, LANES), f32),
        in_specs=[vmem()],
        out_specs=vmem(),
        compiler_params=pltpu.CompilerParams(vmem_limit_bytes=24 << 20),
        name="finish",
    )(near(back))
    full = full.reshape(slabs, rows_b, dof // 2, rows_c, LANES).transpose(0, 1, 3, 2, 4)
    return full.reshape(slabs, rows_b, rows_c, dof // 2 * LANES)


def solution(mesh):
    return jax.shard_map(
        local,
        mesh=mesh,
        in_specs=(
            P("slab", "grp", None, None),
            P("slab", "grp", None, None),
            P("slab", "grp", None, None),
            P("slab", "grp", None, None),
            P(),
            P(),
            P(),
            P("slab", "grp", None, None, None),
        ),
        out_specs=P(None, "grp", None, None),
        check_vma=False,
    )
```

```python
import jax
import jax.numpy as jnp
from jax import lax
from jax.experimental import pallas as pl
from jax.experimental.pallas import tpu as pltpu
from jax.sharding import PartitionSpec as P

SWEEPS = 8
LANES = 128
FACES = 6
PADM = 32
GROUPS = 4

f32 = jnp.float32
bf16 = jnp.bfloat16


def halves(x):
    hi = x.astype(bf16)
    lo = (x - hi.astype(f32)).astype(bf16)
    return hi, lo


def contract0(a, b):
    return lax.dot_general(a, b, (((0,), (0,)), ((), ())), preferred_element_type=f32)


def coarse_kernel(slot_s, dens, slot_v, links, code, prolong, rhs, out, wide, pairs, weights, info):
    kids, dof, _ = prolong.shape
    half = dof // 2
    _, rows_b, rows_c, _ = dens.shape
    count = rows_b * rows_c
    members = out.shape[0]
    groups = half
    info[...] = jnp.zeros(info.shape, f32)
    for a in range(count):
        b, c = a // rows_c, a % rows_c
        info[a : a + 1, 0:kids] = dens[0, b, c : c + 1, :]
        info[a : a + 1, kids : 2 * kids] = slot_v[0, b, c : c + 1, :].astype(f32)
        info[a : a + 1, 2 * kids : 2 * kids + FACES] = jnp.where(
            links[0, b, c : c + 1, :] >= 0, f32(1.0), f32(0.0)
        )
        info[a : a + 1, 3 * kids : 3 * kids + FACES] = code[0, b, c : c + 1, :].astype(f32)
    out[:, count : 2 * count, :] = jnp.broadcast_to(info[0:count, :][None], (members, count, LANES))
    first_half = lax.broadcasted_iota(jnp.int32, (half, LANES), 1) < dof
    for s in range(kids):
        wide[s, :, 0:dof] = prolong[s]
        even = wide[s, pl.ds(0, half, stride=2), :]
        odd = wide[s, pl.ds(1, half, stride=2), :]
        pairs[s] = jnp.where(first_half, even, pltpu.roll(odd, dof, 1))
    for a in range(count):
        b, c = a // rows_c, a % rows_c
        for q in range(kids):
            weights[a, pl.ds(q, half, stride=kids), :] = pairs[slot_s[0, b, c, q]]
    for a in range(count):
        b, c = a // rows_c, a % rows_c
        cells = rhs[0, b, c].astype(f32)
        cells = jnp.concatenate([cells[:, t * LANES : (t + 1) * LANES] for t in range(half)], axis=0)
        hi, lo = halves(weights[a])
        prod = contract0(cells.astype(bf16), jnp.concatenate([hi, lo], axis=1))
        prod = prod[:, :LANES] + prod[:, LANES:]
        own = prod[:dof, :dof] + prod[dof:, dof:]
        row = jnp.concatenate([own[:groups], own[groups:]], axis=1)
        for first in range(0, members, groups):
            out[first : first + groups, a, :] = row


def matrices_kernel(stiffness, prolong, penalty, stacked, columns, mall, extra):
    kids, dof, _ = prolong.shape
    codes = penalty.shape[0]
    half = dof // 2
    rows = dof // GROUPS
    s_hi, s_lo = halves(stiffness[...])
    s_left = jnp.concatenate([s_hi, s_hi, s_lo], axis=1)
    eye = (
        lax.broadcasted_iota(jnp.int32, (dof, dof), 0) == lax.broadcasted_iota(jnp.int32, (dof, dof), 1)
    ).astype(f32)
    extra[...] = jnp.zeros(extra.shape, f32)
    mall[kids + codes :] = jnp.zeros((PADM - kids - codes, half, 2 * dof), f32)
    for m in range(kids + codes):
        if m < kids:
            p_hi, p_lo = halves(prolong[m])
            right = jnp.concatenate([p_hi, p_lo, p_hi], axis=0)
            q_hi, q_lo = halves(jnp.dot(s_left, right, preferred_element_type=f32))
            mat = contract0(
                jnp.concatenate([p_hi, p_hi, p_lo], axis=0), jnp.concatenate([q_hi, q_lo, q_hi], axis=0)
            )
        else:
            mat = penalty[m - kids]
            extra[m : m + 1, dof : 2 * dof] = jnp.sum(jnp.abs(mat), axis=0, keepdims=True)
        extra[m : m + 1, 0:dof] = jnp.sum(mat * eye, axis=0, keepdims=True)
        mall[m, :, 0:dof] = mat[:half]
        mall[m, :, dof : 2 * dof] = mat[half:]
    for pair in range(half + 1):
        both = mall[:, pair, :] if pair < half else extra[...]
        hi, lo = halves(both)
        columns[pair] = jnp.concatenate([hi, hi, lo], axis=0).T
        if pair < half:
            for place in range(2):
                row = pair + place * half
                cut = slice(place * dof, (place + 1) * dof)
                g, first = row // rows, row % rows * (kids + codes)
                stacked[g, first : first + kids + codes, :] = jnp.concatenate(
                    [hi[: kids + codes, cut], hi[: kids + codes, cut], lo[: kids + codes, cut]], axis=1
                )


def solve_kernel(strides, got, stacked, columns, out, flat, resid, update, answer, tiles):
    count = got.shape[1] // 2
    members = got.shape[0]
    total = members * count
    dof = resid.shape[0]
    kids = 8
    rows = dof // GROUPS
    for a in range(count):
        flat[0, pl.ds(a, members, stride=count), :] = got[:, a, :]
        flat[1, pl.ds(a, members, stride=count), :] = got[:, count + a, :]
    coarse = flat[0].T
    facts = flat[1].T
    dens = facts[0:kids]
    slots = facts[kids : 2 * kids]
    open_face = facts[2 * kids : 3 * kids] > 0.5
    codes = facts[3 * kids : 4 * kids].astype(jnp.int32)
    rho = jnp.sum(dens, axis=0, keepdims=True) * f32(1.0 / kids)
    inverse = 1.0 / dens
    place = lax.broadcasted_iota(jnp.int32, (kids, total), 0)
    weight = jnp.zeros((kids, total), f32)
    for q in range(kids):
        weight = weight + jnp.where(slots[q : q + 1] == place.astype(f32), inverse[q : q + 1], 0.0)
    shifts = [sign * stride for stride in strides for sign in (-1, 1)]
    lane = lax.broadcasted_iota(jnp.int32, (kids, total), 1)

    def across(x, flip):
        if total == LANES:
            moved = lane
            for f in range(FACES):
                moved = jnp.where(place == f, lane + shifts[f ^ flip], moved)
            return jnp.take_along_axis(x, moved & (total - 1), axis=1)
        moved = jnp.zeros(x.shape, x.dtype)
        for f in range(FACES):
            moved = jnp.where(place == f, pltpu.roll(x, (-shifts[f ^ flip]) % total, 1), moved)
        return moved

    def pick(x, rows_of):
        return jnp.concatenate(
            [
                jnp.take_along_axis(
                    x[:, t * LANES : (t + 1) * LANES], rows_of[:, t * LANES : (t + 1) * LANES], axis=0
                )
                for t in range(total // LANES)
            ],
            axis=1,
        )

    face_w = jnp.where(open_face, 2.0 / (rho + across(jnp.broadcast_to(rho, (kids, total)), 0)), 0.0)
    code_place = lax.broadcasted_iota(jnp.int32, (16, total), 0)
    face_sum = jnp.zeros((16, total), f32)
    for f in range(FACES):
        face_sum = face_sum + jnp.where(codes[f : f + 1] == code_place, face_w[f : f + 1], 0.0)
    coef = jnp.concatenate([weight, face_sum, jnp.zeros((8, total), f32)], axis=0)
    c_hi, c_lo = halves(coef)
    c_all = jnp.concatenate([c_hi, c_lo, c_hi], axis=0)
    last = jnp.dot(columns[dof // 2], c_all, preferred_element_type=f32)
    jacobi = last[:dof]
    sums = last[dof:]
    for pair in range(dof // 2):
        part = jnp.abs(jnp.dot(columns[pair], c_all, preferred_element_type=f32))
        sums = sums + (part[:dof] + part[dof:])
    upper = jnp.max(jnp.max(sums / jacobi, axis=0, keepdims=True), axis=1, keepdims=True)
    lower = upper / 10.0
    centre = 0.5 * (upper + lower)
    half_width = 0.5 * (upper - lower)
    sigma = centre / half_width
    damping = 1.0 / sigma
    inv_jac = 1.0 / jacobi
    start = jnp.concatenate([coarse[:dof], coarse[dof:]], axis=1)
    resid[...] = start
    start = start * jnp.concatenate([inv_jac, inv_jac], axis=1) / centre
    update[...] = start
    answer[...] = start
    code_row = codes & 7
    upper_half = codes > 7

    def sweep(_, damp):
        hi, lo = halves(update[...])
        right = jnp.concatenate([hi, lo, hi], axis=0)
        damp_next = 1.0 / (2.0 * sigma - damp)
        keep = damp_next * damp
        gain = 2.0 * damp_next / half_width
        for g in range(GROUPS):
            prod = jnp.dot(stacked[g], right, preferred_element_type=f32)
            for first in range(0, rows, 8):
                for c in range(2):
                    cut = slice(c * total, (c + 1) * total)
                    sums = []
                    for n in range(8):
                        base = (first + n) * 24
                        face = jnp.where(
                            upper_half,
                            pick(prod[base + 16 : base + 24, cut], code_row),
                            pick(prod[base + 8 : base + 16, cut], code_row),
                        )
                        face = face * face_w
                        sums.append(prod[base : base + 8, cut] * weight + (face - across(face, 1)))
                    for bit in (4, 2, 1):
                        clear = (place & bit) == 0
                        sums = [
                            jnp.where(clear, sums[n], sums[n + bit])
                            + pick(jnp.where(clear, sums[n + bit], sums[n]), place ^ bit)
                            for n in range(bit)
                        ]
                    part = pl.ds(g * rows + first, 8)
                    left = resid[part, cut] - sums[0]
                    resid[part, cut] = left
                    inv = inv_jac[g * rows + first : g * rows + first + 8]
                    new = keep * update[part, cut] + gain * (left * inv)
                    update[part, cut] = new
                    answer[part, cut] = answer[part, cut] + new
        return damp_next

    lax.fori_loop(0, SWEEPS, sweep, damping)
    grp_count = strides[0] // count
    firsts = total // strides[0]
    half = dof // 2
    lane_tiles = total // LANES
    for t in range(2 * lane_tiles):
        tiles[t] = answer[:, t * LANES : (t + 1) * LANES]
    for low in range(2):
        for c in range(2):
            for t in range(lane_tiles):
                block = tiles[c * lane_tiles + t, pl.ds(low, half, stride=2), :]
                flat[0, t * LANES : (t + 1) * LANES, 0:half] = block.T
            row = jnp.concatenate(
                [flat[0, pl.ds(n, members, stride=count), 0:half] for n in range(count)], axis=1
            )
            for i in range(firsts):
                piece = row[i * grp_count : (i + 1) * grp_count]
                for s in range(members // grp_count):
                    out[pl.ds(s * grp_count, grp_count), (low * 2 + c) * firsts + i, :] = piece


def finish_kernel(got, out):
    firsts = got.shape[1] // 4
    sources = 32
    rows_b, rows_c = 2, 2
    half = 32
    for i in range(firsts):
        block = jnp.concatenate([got[0:sources, x * firsts + i, :] for x in range(4)], axis=0).T
        for n in range(rows_b * rows_c):
            b, c = n // rows_c, n % rows_c
            out[i * rows_b + b, pl.ds(c, half, stride=rows_c), :] = block[n * half : (n + 1) * half]


def vmem():
    return pl.BlockSpec(memory_space=pltpu.VMEM)


def near(x):
    return pltpu.with_memory_space_constraint(x, pltpu.VMEM)


def local(cell_density, cell_slot, neighbours, face_code, stiffness, prolong, penalty, fine_rhs):
    _, rows_b, rows_c, kids = cell_density.shape
    dof = stiffness.shape[0]
    count = rows_b * rows_c
    slabs, grps = lax.axis_size("slab"), lax.axis_size("grp")
    members = slabs * grps
    total = members * count
    every = ("slab", "grp")
    strides = (grps * count, rows_c, 1)
    sent = pl.pallas_call(
        coarse_kernel,
        out_shape=pltpu.VMEM((members, 2 * count, LANES), f32),
        in_specs=[pl.BlockSpec(memory_space=pltpu.SMEM)] + [vmem()] * 6,
        out_specs=vmem(),
        scratch_shapes=[
            pltpu.VMEM((kids, dof, LANES), f32),
            pltpu.VMEM((kids, dof // 2, LANES), f32),
            pltpu.VMEM((count, kids * dof // 2, LANES), f32),
            pltpu.VMEM((8, LANES), f32),
        ],
        name="coarse",
    )(cell_slot, cell_density, cell_slot, neighbours, face_code, prolong, fine_rhs)
    got = lax.all_to_all(sent, every, 0, 0, tiled=True)
    stacked, columns = pl.pallas_call(
        matrices_kernel,
        out_shape=(
            pltpu.VMEM((GROUPS, 24 * (dof // GROUPS), 3 * dof), bf16),
            pltpu.VMEM((dof // 2 + 1, 2 * dof, 3 * PADM), bf16),
        ),
        in_specs=[vmem()] * 3,
        out_specs=(vmem(), vmem()),
        scratch_shapes=[pltpu.VMEM((PADM, dof // 2, 2 * dof), f32), pltpu.VMEM((PADM, 2 * dof), f32)],
        compiler_params=pltpu.CompilerParams(vmem_limit_bytes=24 << 20),
        name="matrices",
    )(near(stiffness), near(prolong), near(penalty))
    back = pl.pallas_call(
        lambda *refs: solve_kernel(strides, *refs),
        out_shape=pltpu.VMEM((members, 4 * slabs, LANES), f32),
        in_specs=[vmem()] * 3,
        out_specs=vmem(),
        scratch_shapes=[
            pltpu.VMEM((2, total, LANES), f32),
            pltpu.VMEM((dof, 2 * total), f32),
            pltpu.VMEM((dof, 2 * total), f32),
            pltpu.VMEM((dof, 2 * total), f32),
            pltpu.VMEM((2 * total // LANES, dof, LANES), f32),
        ],
        compiler_params=pltpu.CompilerParams(vmem_limit_bytes=40 << 20),
        name="solve",
    )(near(got), near(stacked), near(columns))
    back = lax.all_to_all(back, every, 0, 0, tiled=True)
    full = pl.pallas_call(
        finish_kernel,
        out_shape=jax.ShapeDtypeStruct((slabs * rows_b, dof, LANES), f32),
        in_specs=[vmem()],
        out_specs=vmem(),
        compiler_params=pltpu.CompilerParams(vmem_limit_bytes=24 << 20),
        name="finish",
    )(near(back))
    full = full.reshape(slabs, rows_b, dof // 2, rows_c, LANES).transpose(0, 1, 3, 2, 4)
    return full.reshape(slabs, rows_b, rows_c, dof // 2 * LANES)


def solution(mesh):
    return jax.shard_map(
        local,
        mesh=mesh,
        in_specs=(
            P("slab", "grp", None, None),
            P("slab", "grp", None, None),
            P("slab", "grp", None, None),
            P("slab", "grp", None, None),
            P(),
            P(),
            P(),
            P("slab", "grp", None, None, None),
        ),
        out_specs=P(None, "grp", None, None),
        check_vma=False,
    )
```

```python
import jax
import jax.numpy as jnp
from jax import lax
from jax.experimental import pallas as pl
from jax.experimental.pallas import tpu as pltpu
from jax.sharding import PartitionSpec as P

SWEEPS = 8
LANES = 128
FACES = 6
PADM = 32
GROUPS = 4

f32 = jnp.float32
bf16 = jnp.bfloat16


def halves(x):
    hi = x.astype(bf16)
    lo = (x - hi.astype(f32)).astype(bf16)
    return hi, lo


def contract0(a, b):
    return lax.dot_general(a, b, (((0,), (0,)), ((), ())), preferred_element_type=f32)


def coarse_kernel(
    dens_h, slot_h, links_h, code_h, stiffness_h, prolong_h, penalty_h, rhs_h,
    out, stiff, prolong, penalty,
    slot_s, dens, slot_v, links, code, rhs, wide, pairs, weights, info, sems,
):
    moves = [
        pltpu.make_async_copy(source, target, sems.at[n])
        for n, (source, target) in enumerate(
            [
                (prolong_h, prolong),
                (slot_h, slot_s),
                (rhs_h, rhs),
                (dens_h, dens),
                (slot_h, slot_v),
                (links_h, links),
                (code_h, code),
                (penalty_h, penalty),
                (stiffness_h, stiff),
            ]
        )
    ]
    for move in moves:
        move.start()
    kids, dof, _ = prolong.shape
    half = dof // 2
    _, rows_b, rows_c, _ = dens.shape
    count = rows_b * rows_c
    span = count + 1
    members = out.shape[0] // span
    groups = half
    wide_fact = LANES // count
    info[...] = jnp.zeros(info.shape, f32)
    moves[0].wait()
    first_half = lax.broadcasted_iota(jnp.int32, (half, LANES), 1) < dof
    for s in range(kids):
        wide[s, :, 0:dof] = prolong[s]
        even = wide[s, pl.ds(0, half, stride=2), :]
        odd = wide[s, pl.ds(1, half, stride=2), :]
        pairs[s] = jnp.where(first_half, even, pltpu.roll(odd, dof, 1))
    moves[1].wait()
    for a in range(count):
        b, c = a // rows_c, a % rows_c
        for q in range(kids):
            weights[a, pl.ds(q, half, stride=kids), :] = pairs[slot_s[0, b, c, q]]
    for move in moves[2:7]:
        move.wait()
    for a in range(count):
        b, c = a // rows_c, a % rows_c
        base = a * wide_fact
        info[0:1, base : base + kids] = dens[0, b, c : c + 1, :]
        info[0:1, base + kids : base + 2 * kids] = slot_v[0, b, c : c + 1, :].astype(f32)
        info[0:1, base + 2 * kids : base + 2 * kids + FACES] = jnp.where(
            links[0, b, c : c + 1, :] >= 0, f32(1.0), f32(0.0)
        )
        info[0:1, base + 3 * kids : base + 3 * kids + FACES] = code[0, b, c : c + 1, :].astype(f32)
    facts = jnp.broadcast_to(info[0:1, :], (groups, LANES))
    for first in range(0, members, groups):
        out[pl.ds(first * span + count, groups, stride=span), :] = facts
    for a in range(count):
        b, c = a // rows_c, a % rows_c
        cells = rhs[0, b, c].astype(f32)
        cells = jnp.concatenate([cells[:, t * LANES : (t + 1) * LANES] for t in range(half)], axis=0)
        hi, lo = halves(weights[a])
        prod = contract0(cells.astype(bf16), jnp.concatenate([hi, lo], axis=1))
        prod = prod[:, :LANES] + prod[:, LANES:]
        own = prod[:dof, :dof] + prod[dof:, dof:]
        row = jnp.concatenate([own[:groups], own[groups:]], axis=1)
        for first in range(0, members, groups):
            out[pl.ds(first * span + a, groups, stride=span), :] = row
    for move in moves[7:]:
        move.wait()


def matrices_kernel(stiffness, prolong, penalty, stacked, columns, mall, extra):
    kids, dof, _ = prolong.shape
    codes = penalty.shape[0]
    half = dof // 2
    rows = dof // GROUPS
    s_hi, s_lo = halves(stiffness[...])
    s_left = jnp.concatenate([s_hi, s_hi, s_lo], axis=1)
    eye = (
        lax.broadcasted_iota(jnp.int32, (dof, dof), 0) == lax.broadcasted_iota(jnp.int32, (dof, dof), 1)
    ).astype(f32)
    extra[...] = jnp.zeros(extra.shape, f32)
    mall[kids + codes :] = jnp.zeros((PADM - kids - codes, half, 2 * dof), f32)
    for m in range(kids + codes):
        if m < kids:
            p_hi, p_lo = halves(prolong[m])
            right = jnp.concatenate([p_hi, p_lo, p_hi], axis=0)
            q_hi, q_lo = halves(jnp.dot(s_left, right, preferred_element_type=f32))
            mat = contract0(
                jnp.concatenate([p_hi, p_hi, p_lo], axis=0), jnp.concatenate([q_hi, q_lo, q_hi], axis=0)
            )
        else:
            mat = penalty[m - kids]
            extra[m : m + 1, dof : 2 * dof] = jnp.sum(jnp.abs(mat), axis=0, keepdims=True)
        extra[m : m + 1, 0:dof] = jnp.sum(mat * eye, axis=0, keepdims=True)
        mall[m, :, 0:dof] = mat[:half]
        mall[m, :, dof : 2 * dof] = mat[half:]
    parts = []
    for pair in range(half + 1):
        both = mall[:, pair, :] if pair < half else extra[...]
        hi, lo = halves(both)
        parts.append(jnp.concatenate([hi, hi, lo], axis=0))
        if pair % 2:
            columns[pair // 2] = jnp.concatenate(parts[pair - 1 :], axis=0).T
        elif pair == half:
            columns[pair // 2] = jnp.concatenate([parts[pair], jnp.zeros_like(parts[pair])], axis=0).T
        if pair < half:
            for place in range(2):
                row = pair + place * half
                cut = slice(place * dof, (place + 1) * dof)
                g, first = row // rows, row % rows * (kids + codes)
                stacked[g, first : first + kids + codes, :] = jnp.concatenate(
                    [hi[: kids + codes, cut], hi[: kids + codes, cut], lo[: kids + codes, cut]], axis=1
                )


def solve_kernel(strides, got, stacked, columns, out, flat, resid, update, answer, tiles):
    total = flat.shape[1]
    span = got.shape[0] // out.shape[0]
    count = span - 1
    members = out.shape[0]
    wide_fact = LANES // count
    dof = resid.shape[0]
    kids = 8
    rows = dof // GROUPS
    everyone = got[pl.ds(count, members, stride=span), :]
    for a in range(count):
        flat[0, pl.ds(a, members, stride=count), :] = got[pl.ds(a, members, stride=span), :]
        own = pltpu.roll(everyone, LANES - a * wide_fact, 1) if a else everyone
        flat[1, pl.ds(a, members, stride=count), :] = own
    coarse = flat[0].T
    facts = flat[1].T
    dens = facts[0:kids]
    slots = facts[kids : 2 * kids]
    open_face = facts[2 * kids : 3 * kids] > 0.5
    codes = facts[3 * kids : 4 * kids].astype(jnp.int32)
    rho = jnp.sum(dens, axis=0, keepdims=True) * f32(1.0 / kids)
    inverse = 1.0 / dens
    place = lax.broadcasted_iota(jnp.int32, (kids, total), 0)
    weight = jnp.zeros((kids, total), f32)
    for q in range(kids):
        weight = weight + jnp.where(slots[q : q + 1] == place.astype(f32), inverse[q : q + 1], 0.0)
    shifts = [sign * stride for stride in strides for sign in (-1, 1)]
    lane = lax.broadcasted_iota(jnp.int32, (kids, total), 1)

    def across(x, flip):
        if total == LANES:
            moved = lane
            for f in range(FACES):
                moved = jnp.where(place == f, lane + shifts[f ^ flip], moved)
            return jnp.take_along_axis(x, moved & (total - 1), axis=1)
        moved = jnp.zeros(x.shape, x.dtype)
        for f in range(FACES):
            moved = jnp.where(place == f, pltpu.roll(x, (-shifts[f ^ flip]) % total, 1), moved)
        return moved

    def pick(x, rows_of):
        return jnp.concatenate(
            [
                jnp.take_along_axis(
                    x[:, t * LANES : (t + 1) * LANES], rows_of[:, t * LANES : (t + 1) * LANES], axis=0
                )
                for t in range(total // LANES)
            ],
            axis=1,
        )

    face_w = jnp.where(open_face, 2.0 / (rho + across(jnp.broadcast_to(rho, (kids, total)), 0)), 0.0)
    code_place = lax.broadcasted_iota(jnp.int32, (16, total), 0)
    face_sum = jnp.zeros((16, total), f32)
    for f in range(FACES):
        face_sum = face_sum + jnp.where(codes[f : f + 1] == code_place, face_w[f : f + 1], 0.0)
    coef = jnp.concatenate([weight, face_sum, jnp.zeros((8, total), f32)], axis=0)
    c_hi, c_lo = halves(coef)
    c_all = jnp.concatenate([c_hi, c_lo, c_hi], axis=0)
    nothing = jnp.zeros_like(c_all)
    c_two = jnp.concatenate(
        [jnp.concatenate([c_all, nothing], axis=1), jnp.concatenate([nothing, c_all], axis=1)], axis=0
    )
    last = jnp.dot(columns[dof // 4], c_two, preferred_element_type=f32)
    jacobi = last[:dof, :total]
    sums = last[dof:, :total]
    for pair in range(dof // 4):
        part = jnp.abs(jnp.dot(columns[pair], c_two, preferred_element_type=f32))
        part = part[:dof] + part[dof:]
        sums = sums + (part[:, :total] + part[:, total:])
    upper = jnp.max(jnp.max(sums / jacobi, axis=0, keepdims=True), axis=1, keepdims=True)
    lower = upper / 10.0
    centre = 0.5 * (upper + lower)
    half_width = 0.5 * (upper - lower)
    sigma = centre / half_width
    damping = 1.0 / sigma
    inv_jac = 1.0 / jacobi
    start = jnp.concatenate([coarse[:dof], coarse[dof:]], axis=1)
    resid[...] = start
    start = start * jnp.concatenate([inv_jac, inv_jac], axis=1) / centre
    update[...] = start
    answer[...] = start
    code_row = codes & 7
    upper_half = codes > 7

    def sweep(_, damp):
        hi, lo = halves(update[...])
        right = jnp.concatenate([hi, lo, hi], axis=0)
        damp_next = 1.0 / (2.0 * sigma - damp)
        keep = damp_next * damp
        gain = 2.0 * damp_next / half_width
        for g in range(GROUPS):
            prod = jnp.dot(stacked[g], right, preferred_element_type=f32)
            for first in range(0, rows, 8):
                for c in range(2):
                    cut = slice(c * total, (c + 1) * total)
                    sums = []
                    for n in range(8):
                        base = (first + n) * 24
                        face = jnp.where(
                            upper_half,
                            pick(prod[base + 16 : base + 24, cut], code_row),
                            pick(prod[base + 8 : base + 16, cut], code_row),
                        )
                        face = face * face_w
                        sums.append(prod[base : base + 8, cut] * weight + (face - across(face, 1)))
                    for bit in (4, 2, 1):
                        clear = (place & bit) == 0
                        sums = [
                            jnp.where(clear, sums[n], sums[n + bit])
                            + pick(jnp.where(clear, sums[n + bit], sums[n]), place ^ bit)
                            for n in range(bit)
                        ]
                    part = pl.ds(g * rows + first, 8)
                    left = resid[part, cut] - sums[0]
                    resid[part, cut] = left
                    inv = inv_jac[g * rows + first : g * rows + first + 8]
                    new = keep * update[part, cut] + gain * (left * inv)
                    update[part, cut] = new
                    answer[part, cut] = answer[part, cut] + new
        return damp_next

    lax.fori_loop(0, SWEEPS, sweep, damping)
    grp_count = strides[0] // count
    firsts = total // strides[0]
    half = dof // 2
    lane_tiles = total // LANES
    for t in range(2 * lane_tiles):
        tiles[t] = answer[:, t * LANES : (t + 1) * LANES]
    for low in range(2):
        for c in range(2):
            for t in range(lane_tiles):
                block = tiles[c * lane_tiles + t, pl.ds(low, half, stride=2), :]
                flat[0, t * LANES : (t + 1) * LANES, 0:half] = block.T
            row = jnp.concatenate(
                [flat[0, pl.ds(n, members, stride=count), 0:half] for n in range(count)], axis=1
            )
            for i in range(firsts):
                piece = row[i * grp_count : (i + 1) * grp_count]
                for s in range(members // grp_count):
                    out[pl.ds(s * grp_count, grp_count), (low * 2 + c) * firsts + i, :] = piece


def finish_kernel(got, out):
    firsts = got.shape[1] // 4
    sources = 32
    rows_b, rows_c = 2, 2
    half = 32
    for i in range(firsts):
        block = jnp.concatenate([got[0:sources, x * firsts + i, :] for x in range(4)], axis=0).T
        for n in range(rows_b * rows_c):
            b, c = n // rows_c, n % rows_c
            out[i * rows_b + b, pl.ds(c, half, stride=rows_c), :] = block[n * half : (n + 1) * half]


def vmem():
    return pl.BlockSpec(memory_space=pltpu.VMEM)


def near(x):
    return pltpu.with_memory_space_constraint(x, pltpu.VMEM)


def local(cell_density, cell_slot, neighbours, face_code, stiffness, prolong, penalty, fine_rhs):
    _, rows_b, rows_c, kids = cell_density.shape
    dof = stiffness.shape[0]
    count = rows_b * rows_c
    slabs, grps = lax.axis_size("slab"), lax.axis_size("grp")
    members = slabs * grps
    total = members * count
    every = ("slab", "grp")
    strides = (grps * count, rows_c, 1)
    anywhere = pl.BlockSpec(memory_space=pl.ANY)
    codes = penalty.shape[0]
    sent, stiff, prol, pen = pl.pallas_call(
        coarse_kernel,
        out_shape=(
            pltpu.HBM((members * (count + 1), LANES), f32),
            pltpu.VMEM((dof, dof), f32),
            pltpu.VMEM((kids, dof, dof), f32),
            pltpu.VMEM((codes, dof, dof), f32),
        ),
        in_specs=[anywhere] * 8,
        out_specs=(vmem(), vmem(), vmem(), vmem()),
        scratch_shapes=[
            pltpu.SMEM(cell_slot.shape, jnp.int32),
            pltpu.VMEM(cell_density.shape, f32),
            pltpu.VMEM(cell_slot.shape, jnp.int32),
            pltpu.VMEM(neighbours.shape, jnp.int32),
            pltpu.VMEM(face_code.shape, jnp.int32),
            pltpu.VMEM(fine_rhs.shape, bf16),
            pltpu.VMEM((kids, dof, LANES), f32),
            pltpu.VMEM((kids, dof // 2, LANES), f32),
            pltpu.VMEM((count, kids * dof // 2, LANES), f32),
            pltpu.VMEM((8, LANES), f32),
            pltpu.SemaphoreType.DMA((9,)),
        ],
        compiler_params=pltpu.CompilerParams(vmem_limit_bytes=24 << 20),
        name="coarse",
    )(
        *[
            pltpu.with_memory_space_constraint(x, pltpu.HBM)
            for x in (cell_density, cell_slot, neighbours, face_code, stiffness, prolong, penalty, fine_rhs)
        ]
    )
    got = lax.all_to_all(sent.reshape(members, 1, (count + 1) * LANES), every, 0, 0, tiled=True)
    got = got.reshape(members * (count + 1), LANES)
    stacked, columns = pl.pallas_call(
        matrices_kernel,
        out_shape=(
            pltpu.VMEM((GROUPS, 24 * (dof // GROUPS), 3 * dof), bf16),
            pltpu.VMEM((dof // 4 + 1, 2 * dof, 6 * PADM), bf16),
        ),
        in_specs=[vmem()] * 3,
        out_specs=(vmem(), vmem()),
        scratch_shapes=[pltpu.VMEM((PADM, dof // 2, 2 * dof), f32), pltpu.VMEM((PADM, 2 * dof), f32)],
        compiler_params=pltpu.CompilerParams(vmem_limit_bytes=24 << 20),
        name="matrices",
    )(near(stiff), near(prol), near(pen))
    back = pl.pallas_call(
        lambda *refs: solve_kernel(strides, *refs),
        out_shape=pltpu.VMEM((members, 4 * slabs, LANES), f32),
        in_specs=[vmem()] * 3,
        out_specs=vmem(),
        scratch_shapes=[
            pltpu.VMEM((2, total, LANES), f32),
            pltpu.VMEM((dof, 2 * total), f32),
            pltpu.VMEM((dof, 2 * total), f32),
            pltpu.VMEM((dof, 2 * total), f32),
            pltpu.VMEM((2 * total // LANES, dof, LANES), f32),
        ],
        compiler_params=pltpu.CompilerParams(vmem_limit_bytes=40 << 20),
        name="solve",
    )(near(got), near(stacked), near(columns))
    back = lax.all_to_all(back, every, 0, 0, tiled=True)
    full = pl.pallas_call(
        finish_kernel,
        out_shape=jax.ShapeDtypeStruct((slabs * rows_b, dof, LANES), f32),
        in_specs=[vmem()],
        out_specs=vmem(),
        compiler_params=pltpu.CompilerParams(vmem_limit_bytes=24 << 20),
        name="finish",
    )(near(back))
    full = full.reshape(slabs, rows_b, dof // 2, rows_c, LANES).transpose(0, 1, 3, 2, 4)
    return full.reshape(slabs, rows_b, rows_c, dof // 2 * LANES)


def solution(mesh):
    return jax.shard_map(
        local,
        mesh=mesh,
        in_specs=(
            P("slab", "grp", None, None),
            P("slab", "grp", None, None),
            P("slab", "grp", None, None),
            P("slab", "grp", None, None),
            P(),
            P(),
            P(),
            P("slab", "grp", None, None, None),
        ),
        out_specs=P(None, "grp", None, None),
        check_vma=False,
    )
```

```python
import jax
import jax.numpy as jnp
from jax import lax
from jax.experimental import pallas as pl
from jax.experimental.pallas import tpu as pltpu
from jax.sharding import PartitionSpec as P

SWEEPS = 8
LANES = 128
FACES = 6
PADM = 32
GROUPS = 4

f32 = jnp.float32
bf16 = jnp.bfloat16


def halves(x):
    hi = x.astype(bf16)
    lo = (x - hi.astype(f32)).astype(bf16)
    return hi, lo


def contract0(a, b):
    return lax.dot_general(a, b, (((0,), (0,)), ((), ())), preferred_element_type=f32)


def coarse_kernel(
    dens_h, slot_h, links_h, code_h, stiffness_h, prolong_h, penalty_h, rhs_h,
    out, stiff, prolong, penalty,
    slot_s, dens, slot_v, links, code, rhs, wide, pairs, weights, info, sems,
):
    moves = [
        pltpu.make_async_copy(source, target, sems.at[n])
        for n, (source, target) in enumerate(
            [
                (prolong_h, prolong),
                (slot_h, slot_s),
                (rhs_h, rhs),
                (dens_h, dens),
                (slot_h, slot_v),
                (links_h, links),
                (code_h, code),
                (penalty_h, penalty),
                (stiffness_h, stiff),
            ]
        )
    ]
    for move in moves:
        move.start()
    kids, dof, _ = prolong.shape
    half = dof // 2
    _, rows_b, rows_c, _ = dens.shape
    count = rows_b * rows_c
    span = count + 1
    members = out.shape[0] // span
    groups = half
    wide_fact = LANES // count
    info[...] = jnp.zeros(info.shape, f32)
    moves[0].wait()
    first_half = lax.broadcasted_iota(jnp.int32, (half, LANES), 1) < dof
    for s in range(kids):
        wide[s, :, 0:dof] = prolong[s]
        even = wide[s, pl.ds(0, half, stride=2), :]
        odd = wide[s, pl.ds(1, half, stride=2), :]
        pairs[s] = jnp.where(first_half, even, pltpu.roll(odd, dof, 1))
    moves[1].wait()
    for a in range(count):
        b, c = a // rows_c, a % rows_c
        for q in range(kids):
            weights[a, pl.ds(q, half, stride=kids), :] = pairs[slot_s[0, b, c, q]]
    for move in moves[2:7]:
        move.wait()
    for a in range(count):
        b, c = a // rows_c, a % rows_c
        base = a * wide_fact
        info[0:1, base : base + kids] = dens[0, b, c : c + 1, :]
        info[0:1, base + kids : base + 2 * kids] = slot_v[0, b, c : c + 1, :].astype(f32)
        info[0:1, base + 2 * kids : base + 2 * kids + FACES] = jnp.where(
            links[0, b, c : c + 1, :] >= 0, f32(1.0), f32(0.0)
        )
        info[0:1, base + 3 * kids : base + 3 * kids + FACES] = code[0, b, c : c + 1, :].astype(f32)
    facts = jnp.broadcast_to(info[0:1, :], (groups, LANES))
    for first in range(0, members, groups):
        out[pl.ds(first * span + count, groups, stride=span), :] = facts
    for a in range(count):
        b, c = a // rows_c, a % rows_c
        cells = rhs[0, b, c].astype(f32)
        cells = jnp.concatenate([cells[:, t * LANES : (t + 1) * LANES] for t in range(half)], axis=0)
        hi, lo = halves(weights[a])
        prod = contract0(cells.astype(bf16), jnp.concatenate([hi, lo], axis=1))
        prod = prod[:, :LANES] + prod[:, LANES:]
        own = prod[:dof, :dof] + prod[dof:, dof:]
        row = jnp.concatenate([own[:groups], own[groups:]], axis=1)
        for first in range(0, members, groups):
            out[pl.ds(first * span + a, groups, stride=span), :] = row
    for move in moves[7:]:
        move.wait()


def matrices_kernel(stiffness, prolong, penalty, stacked, columns, mall, extra):
    kids, dof, _ = prolong.shape
    codes = penalty.shape[0]
    half = dof // 2
    rows = dof // GROUPS
    s_hi, s_lo = halves(stiffness[...])
    s_left = jnp.concatenate([s_hi, s_hi, s_lo], axis=1)
    eye = (
        lax.broadcasted_iota(jnp.int32, (dof, dof), 0) == lax.broadcasted_iota(jnp.int32, (dof, dof), 1)
    ).astype(f32)
    extra[...] = jnp.zeros(extra.shape, f32)
    mall[kids + codes :] = jnp.zeros((PADM - kids - codes, half, 2 * dof), f32)
    for m in range(kids + codes):
        if m < kids:
            p_hi, p_lo = halves(prolong[m])
            right = jnp.concatenate([p_hi, p_lo, p_hi], axis=0)
            q_hi, q_lo = halves(jnp.dot(s_left, right, preferred_element_type=f32))
            mat = contract0(
                jnp.concatenate([p_hi, p_hi, p_lo], axis=0), jnp.concatenate([q_hi, q_lo, q_hi], axis=0)
            )
        else:
            mat = penalty[m - kids]
            extra[m : m + 1, dof : 2 * dof] = jnp.sum(jnp.abs(mat), axis=0, keepdims=True)
        extra[m : m + 1, 0:dof] = jnp.sum(mat * eye, axis=0, keepdims=True)
        mall[m, :, 0:dof] = mat[:half]
        mall[m, :, dof : 2 * dof] = mat[half:]
    parts = []
    for pair in range(half + 1):
        both = mall[:, pair, :] if pair < half else extra[...]
        hi, lo = halves(both)
        parts.append(jnp.concatenate([hi, hi, lo], axis=0))
        if pair % 2:
            columns[pair // 2] = jnp.concatenate(parts[pair - 1 :], axis=0).T
        elif pair == half:
            columns[pair // 2] = jnp.concatenate([parts[pair], jnp.zeros_like(parts[pair])], axis=0).T
        if pair < half:
            for place in range(2):
                row = pair + place * half
                cut = slice(place * dof, (place + 1) * dof)
                g, first = row // rows, row % rows * (kids + codes)
                stacked[g, first : first + kids + codes, :] = jnp.concatenate(
                    [hi[: kids + codes, cut], hi[: kids + codes, cut], lo[: kids + codes, cut]], axis=1
                )


def solve_kernel(strides, got, stacked, columns, out, flat, resid, update, answer, tiles):
    total = flat.shape[1]
    span = got.shape[0] // out.shape[0]
    count = span - 1
    members = out.shape[0]
    wide_fact = LANES // count
    dof = resid.shape[0]
    kids = 8
    rows = dof // GROUPS
    everyone = got[pl.ds(count, members, stride=span), :]
    for a in range(count):
        flat[0, pl.ds(a, members, stride=count), :] = got[pl.ds(a, members, stride=span), :]
        own = pltpu.roll(everyone, LANES - a * wide_fact, 1) if a else everyone
        flat[1, pl.ds(a, members, stride=count), :] = own
    coarse = flat[0].T
    facts = flat[1].T
    dens = facts[0:kids]
    slots = facts[kids : 2 * kids]
    open_face = facts[2 * kids : 3 * kids] > 0.5
    codes = facts[3 * kids : 4 * kids].astype(jnp.int32)
    rho = jnp.sum(dens, axis=0, keepdims=True) * f32(1.0 / kids)
    inverse = 1.0 / dens
    place = lax.broadcasted_iota(jnp.int32, (kids, total), 0)
    weight = jnp.zeros((kids, total), f32)
    for q in range(kids):
        weight = weight + jnp.where(slots[q : q + 1] == place.astype(f32), inverse[q : q + 1], 0.0)
    shifts = [sign * stride for stride in strides for sign in (-1, 1)]
    lane = lax.broadcasted_iota(jnp.int32, (kids, total), 1)

    def across(x, flip):
        if total == LANES:
            moved = lane
            for f in range(FACES):
                moved = jnp.where(place == f, lane + shifts[f ^ flip], moved)
            return jnp.take_along_axis(x, moved & (total - 1), axis=1)
        moved = jnp.zeros(x.shape, x.dtype)
        for f in range(FACES):
            moved = jnp.where(place == f, pltpu.roll(x, (-shifts[f ^ flip]) % total, 1), moved)
        return moved

    def pick(x, rows_of):
        return jnp.concatenate(
            [
                jnp.take_along_axis(
                    x[:, t * LANES : (t + 1) * LANES], rows_of[:, t * LANES : (t + 1) * LANES], axis=0
                )
                for t in range(total // LANES)
            ],
            axis=1,
        )

    face_w = jnp.where(open_face, 2.0 / (rho + across(jnp.broadcast_to(rho, (kids, total)), 0)), 0.0)
    code_place = lax.broadcasted_iota(jnp.int32, (16, total), 0)
    face_sum = jnp.zeros((16, total), f32)
    for f in range(FACES):
        face_sum = face_sum + jnp.where(codes[f : f + 1] == code_place, face_w[f : f + 1], 0.0)
    coef = jnp.concatenate([weight, face_sum, jnp.zeros((8, total), f32)], axis=0)
    c_hi, c_lo = halves(coef)
    c_all = jnp.concatenate([c_hi, c_lo, c_hi], axis=0)
    nothing = jnp.zeros_like(c_all)
    c_two = jnp.concatenate(
        [jnp.concatenate([c_all, nothing], axis=1), jnp.concatenate([nothing, c_all], axis=1)], axis=0
    )
    last = jnp.dot(columns[dof // 4], c_two, preferred_element_type=f32)
    jacobi = last[:dof, :total]
    sums = last[dof:, :total]
    for pair in range(dof // 4):
        part = jnp.abs(jnp.dot(columns[pair], c_two, preferred_element_type=f32))
        part = part[:dof] + part[dof:]
        sums = sums + (part[:, :total] + part[:, total:])
    upper = jnp.max(jnp.max(sums / jacobi, axis=0, keepdims=True), axis=1, keepdims=True)
    inv_jac = 1.0 / (jacobi * upper)
    sigma = 11.0 / 9.0
    start = jnp.concatenate([coarse[:dof], coarse[dof:]], axis=1)
    resid[...] = start
    start = start * jnp.concatenate([inv_jac, inv_jac], axis=1) * f32(1.0 / 0.55)
    update[...] = start
    answer[...] = start
    code_row = codes & 7
    upper_half = codes > 7

    def sweep(keep, gain):
        hi, lo = halves(update[...])
        right = jnp.concatenate([hi, lo, hi], axis=0)
        for g in range(GROUPS):
            prod = jnp.dot(stacked[g], right, preferred_element_type=f32)
            for first in range(0, rows, 8):
                for c in range(2):
                    cut = slice(c * total, (c + 1) * total)
                    sums = []
                    for n in range(8):
                        base = (first + n) * 24
                        face = jnp.where(
                            upper_half,
                            pick(prod[base + 16 : base + 24, cut], code_row),
                            pick(prod[base + 8 : base + 16, cut], code_row),
                        )
                        face = face * face_w
                        sums.append(prod[base : base + 8, cut] * weight + (face - across(face, 1)))
                    for bit in (4, 2, 1):
                        clear = (place & bit) == 0
                        sums = [
                            jnp.where(clear, sums[n], sums[n + bit])
                            + pick(jnp.where(clear, sums[n + bit], sums[n]), place ^ bit)
                            for n in range(bit)
                        ]
                    part = pl.ds(g * rows + first, 8)
                    left = resid[part, cut] - sums[0]
                    resid[part, cut] = left
                    inv = inv_jac[g * rows + first : g * rows + first + 8]
                    new = keep * update[part, cut] + gain * (left * inv)
                    update[part, cut] = new
                    answer[part, cut] = answer[part, cut] + new

    def step(_, damp):
        damp_next = 1.0 / (f32(2.0 * sigma) - damp)
        sweep(damp_next * damp, damp_next * f32(2.0 / 0.45))
        return damp_next

    if total == LANES:
        damp = 1.0 / sigma
        for _ in range(SWEEPS):
            damp_next = 1.0 / (2.0 * sigma - damp)
            sweep(f32(damp_next * damp), f32(2.0 * damp_next / 0.45))
            damp = damp_next
    else:
        lax.fori_loop(0, SWEEPS, step, jnp.full((1, 1), 1.0 / sigma, f32))
    grp_count = strides[0] // count
    firsts = total // strides[0]
    half = dof // 2
    lane_tiles = total // LANES
    for t in range(2 * lane_tiles):
        tiles[t] = answer[:, t * LANES : (t + 1) * LANES]
    for low in range(2):
        for c in range(2):
            for t in range(lane_tiles):
                block = tiles[c * lane_tiles + t, pl.ds(low, half, stride=2), :]
                flat[0, t * LANES : (t + 1) * LANES, 0:half] = block.T
            row = jnp.concatenate(
                [flat[0, pl.ds(n, members, stride=count), 0:half] for n in range(count)], axis=1
            )
            for i in range(firsts):
                piece = row[i * grp_count : (i + 1) * grp_count]
                for s in range(members // grp_count):
                    out[pl.ds(s * grp_count, grp_count), (low * 2 + c) * firsts + i, :] = piece


def finish_kernel(got, out):
    firsts = got.shape[1] // 4
    sources = 32
    rows_b, rows_c = 2, 2
    half = 32
    for i in range(firsts):
        block = jnp.concatenate([got[0:sources, x * firsts + i, :] for x in range(4)], axis=0).T
        for n in range(rows_b * rows_c):
            b, c = n // rows_c, n % rows_c
            out[i * rows_b + b, pl.ds(c, half, stride=rows_c), :] = block[n * half : (n + 1) * half]


def vmem():
    return pl.BlockSpec(memory_space=pltpu.VMEM)


def near(x):
    return pltpu.with_memory_space_constraint(x, pltpu.VMEM)


def local(cell_density, cell_slot, neighbours, face_code, stiffness, prolong, penalty, fine_rhs):
    _, rows_b, rows_c, kids = cell_density.shape
    dof = stiffness.shape[0]
    count = rows_b * rows_c
    slabs, grps = lax.axis_size("slab"), lax.axis_size("grp")
    members = slabs * grps
    total = members * count
    every = ("slab", "grp")
    strides = (grps * count, rows_c, 1)
    anywhere = pl.BlockSpec(memory_space=pl.ANY)
    codes = penalty.shape[0]
    sent, stiff, prol, pen = pl.pallas_call(
        coarse_kernel,
        out_shape=(
            pltpu.HBM((members * (count + 1), LANES), f32),
            pltpu.VMEM((dof, dof), f32),
            pltpu.VMEM((kids, dof, dof), f32),
            pltpu.VMEM((codes, dof, dof), f32),
        ),
        in_specs=[anywhere] * 8,
        out_specs=(vmem(), vmem(), vmem(), vmem()),
        scratch_shapes=[
            pltpu.SMEM(cell_slot.shape, jnp.int32),
            pltpu.VMEM(cell_density.shape, f32),
            pltpu.VMEM(cell_slot.shape, jnp.int32),
            pltpu.VMEM(neighbours.shape, jnp.int32),
            pltpu.VMEM(face_code.shape, jnp.int32),
            pltpu.VMEM(fine_rhs.shape, bf16),
            pltpu.VMEM((kids, dof, LANES), f32),
            pltpu.VMEM((kids, dof // 2, LANES), f32),
            pltpu.VMEM((count, kids * dof // 2, LANES), f32),
            pltpu.VMEM((8, LANES), f32),
            pltpu.SemaphoreType.DMA((9,)),
        ],
        compiler_params=pltpu.CompilerParams(vmem_limit_bytes=24 << 20),
        name="coarse",
    )(
        *[
            pltpu.with_memory_space_constraint(x, pltpu.HBM)
            for x in (cell_density, cell_slot, neighbours, face_code, stiffness, prolong, penalty, fine_rhs)
        ]
    )
    got = lax.all_to_all(sent.reshape(members, 1, (count + 1) * LANES), every, 0, 0, tiled=True)
    got = got.reshape(members * (count + 1), LANES)
    stacked, columns = pl.pallas_call(
        matrices_kernel,
        out_shape=(
            pltpu.VMEM((GROUPS, 24 * (dof // GROUPS), 3 * dof), bf16),
            pltpu.VMEM((dof // 4 + 1, 2 * dof, 6 * PADM), bf16),
        ),
        in_specs=[vmem()] * 3,
        out_specs=(vmem(), vmem()),
        scratch_shapes=[pltpu.VMEM((PADM, dof // 2, 2 * dof), f32), pltpu.VMEM((PADM, 2 * dof), f32)],
        compiler_params=pltpu.CompilerParams(vmem_limit_bytes=24 << 20),
        name="matrices",
    )(near(stiff), near(prol), near(pen))
    back = pl.pallas_call(
        lambda *refs: solve_kernel(strides, *refs),
        out_shape=pltpu.VMEM((members, 4 * slabs, LANES), f32),
        in_specs=[vmem()] * 3,
        out_specs=vmem(),
        scratch_shapes=[
            pltpu.VMEM((2, total, LANES), f32),
            pltpu.VMEM((dof, 2 * total), f32),
            pltpu.VMEM((dof, 2 * total), f32),
            pltpu.VMEM((dof, 2 * total), f32),
            pltpu.VMEM((2 * total // LANES, dof, LANES), f32),
        ],
        compiler_params=pltpu.CompilerParams(vmem_limit_bytes=40 << 20),
        name="solve",
    )(near(got), near(stacked), near(columns))
    back = lax.all_to_all(back, every, 0, 0, tiled=True)
    full = pl.pallas_call(
        finish_kernel,
        out_shape=jax.ShapeDtypeStruct((slabs * rows_b, dof, LANES), f32),
        in_specs=[vmem()],
        out_specs=vmem(),
        compiler_params=pltpu.CompilerParams(vmem_limit_bytes=24 << 20),
        name="finish",
    )(near(back))
    full = full.reshape(slabs, rows_b, dof // 2, rows_c, LANES).transpose(0, 1, 3, 2, 4)
    return full.reshape(slabs, rows_b, rows_c, dof // 2 * LANES)


def solution(mesh):
    return jax.shard_map(
        local,
        mesh=mesh,
        in_specs=(
            P("slab", "grp", None, None),
            P("slab", "grp", None, None),
            P("slab", "grp", None, None),
            P("slab", "grp", None, None),
            P(),
            P(),
            P(),
            P("slab", "grp", None, None, None),
        ),
        out_specs=P(None, "grp", None, None),
        check_vma=False,
    )
```
